32 devices in a mesh: var: 16 (over z, y, core), smp: 2 (over x).
Axes of the slice: x: 2, y: 2, z: 4, core: 2. Of those that a mesh axis runs over, the one named last changes fastest.
Arguments:
- genotype: bfloat16 [32768, 2048], P('var', 'smp'), may hold values from 0 to 2
- labels: int32 [32768], P('var'), may hold values from 0 to 7, as said below
- probes: bfloat16 [20, 2048], P(None, 'smp'), may hold values from -6 to 6
- phenotype: bfloat16 [2048], P('smp'), may hold values from -6 to 6
Outputs:
- moments: float32 [8, 21, 2, 1024], P(None, None, 'smp', 'var')
The draws below stay inside these ranges and needn't reach their ends.
Inputs may be any that keep to these rules, and one draw needn't show every extreme that they name: Within each aligned block of 2048 variants the labels never fall, and every one of the 8 components appears in every block.
All inputs are finite; a program needn't handle non-finite values.
Results may differ from the reference program's by a relative error of at most 0.0039.
Values sent between devices are 32-bit elements; how exact they have to be, the bound alone decides.
A program may use at most 64 MiB of HBM per device.

```python
import math
import jax
import jax.numpy as jnp
from jax import lax

VDEV = 2048
NB = 20
K = 8
NV = 21
M = 32768
R = 1024
Q = 2
N = 2048


def draw_genotype(key, part):
    first, second, third = jax.random.split(jax.random.fold_in(key, 11), 3)
    base = jax.random.uniform(first, (M, 1), jnp.float32, 0.0, 0.7)
    width = jnp.exp(jax.random.uniform(second, (M, 1), jnp.float32, math.log(0.08), math.log(0.9)))
    noise = jax.random.uniform(third, (M, N), jnp.float32)
    return (base + width * noise).astype(jnp.bfloat16)


def draw_labels(key, part):
    first, second = jax.random.split(jax.random.fold_in(key, 23), 2)
    blocks = M // VDEV
    span = max(blocks - 1, 1)
    place = jnp.arange(blocks, dtype=jnp.int32)[:, None]
    comp = jnp.arange(8, dtype=jnp.int32)[None, :]
    rising = span + 3 * place
    falling = 4 * span - 3 * place
    base_weight = jnp.where(comp % 2 == 0, rising, falling)
    jitter = jax.random.randint(second, (blocks, 8), 0, span // 2 + 1)
    cumulative = jnp.cumsum(base_weight + jitter, axis=1).astype(jnp.int32)
    whole = cumulative[:, 7:8]
    raw = jax.random.randint(first, (blocks, VDEV), 0, whole)
    level = jnp.sum((raw[:, :, None] >= cumulative[:, None, :]).astype(jnp.int32), axis=2)
    position = jnp.arange(VDEV, dtype=jnp.int32)[None, :]
    level = jnp.where(position < 8, position % 8, level)
    return jnp.sort(level, axis=1).reshape(M).astype(jnp.int32)


def level_of(rng, extent, shards, smallest, largest):
    factor_of, own = 1.0, jax.random.fold_in(rng, 6)
    for dim, shards_of in shards:
        steps = jnp.exp(jax.random.uniform(jax.random.fold_in(own, dim), (shards_of,), jnp.float32, smallest / len(shards), largest / len(shards)))
        factor_of = factor_of * jnp.repeat(steps, extent[dim] // shards_of).reshape([-1 if axis == dim else 1 for axis in range(len(extent))])
    return factor_of


def centred(rng, dims, scale, limit, cuts=(), held_as=jnp.bfloat16):
    gain = level_of(rng, dims, cuts, -0.22, 0.18) if cuts else 1.0
    values = jax.random.normal(rng, dims, jnp.float32) * scale * gain
    return jnp.minimum(jnp.maximum(values, -limit), limit).astype(held_as)


def setup_inputs(seed: int = 0) -> dict:
    keys = jax.random.split(jax.random.key(seed), 5)
    genotype = draw_genotype(jax.random.fold_in(keys[4], 71), 0)
    labels = draw_labels(jax.random.fold_in(keys[4], 71), 0)
    probes = centred(keys[2], (NB, N), 1.0, 6.0, ((1, 2),))
    phenotype = centred(keys[3], (N,), 1.0, 6.0, ((0, 2),))
    return {"genotype": genotype, "labels": labels, "probes": probes, "phenotype": phenotype}


EPS = 1e-06

def reference(genotype, labels, probes, phenotype):
    vectors = jnp.concatenate([probes, phenotype[None, :]], axis=0)
    member = (labels[None, :] == jnp.arange(K, dtype=jnp.int32)[:, None]).astype(jnp.float32)
    counts = lax.optimization_barrier(jnp.sum(member, axis=1))
    blocks = M // VDEV

    def step(carry, index):
        start = (index * VDEV).astype(jnp.int32)
        dosage = lax.dynamic_slice_in_dim(genotype, start, VDEV, 0).astype(jnp.float32)
        mean = lax.optimization_barrier(jnp.sum(dosage, axis=1)) / N
        centered = dosage - mean[:, None]
        spread = lax.optimization_barrier(jnp.sum(centered * centered, axis=1)) / N
        scaled = (centered * lax.rsqrt(spread + EPS)[:, None]).astype(jnp.bfloat16)
        projected = lax.dot_general(vectors, scaled, (((1,), (1,)), ((), ())), preferred_element_type=jnp.float32)
        local_member = lax.dynamic_slice_in_dim(member, start, VDEV, 1)
        weights = (projected[None, :, :] * local_member[:, None, :] / counts[:, None, None]).astype(jnp.bfloat16)
        weights = weights.reshape(K * NV, VDEV)
        return (carry + jnp.dot(weights, scaled, preferred_element_type=jnp.float32), None)
    start_value = jnp.zeros((K * NV, N), jnp.float32)
    total, unused = lax.scan(step, start_value, jnp.arange(blocks, dtype=jnp.int32))
    return total.reshape(K, NV, Q, R)
```

```python
import functools

import jax
import jax.numpy as jnp
from jax import lax
from jax.experimental import pallas as pl
from jax.experimental.pallas import tpu as pltpu
from jax.sharding import PartitionSpec as P

K = 8
EPS = 1e-06
LANES = 128
CHUNK = 256
MESH = pl.DeviceIdType.MESH


def reverse_bits(value, bits):
    out = 0
    for _ in range(bits):
        out = (out << 1) | (value & 1)
        value >>= 1
    return out


def kernel(nsmp, nvar, g_hbm, lab_ref, probes_ref, phen_ref, out_ref, *scratch):
    levels = (nvar // 2).bit_length() - 1
    tiles = nvar // 2
    (g, vec, psend, precv, vsend, vrecv, w, corr, buf, crecv) = scratch[:10]
    srcs = scratch[10 : 10 + levels]
    keeps = scratch[10 + levels : 10 + 2 * levels]
    recvs = scratch[10 + 2 * levels : 10 + 3 * levels]
    (gsem, p_s, p_r, v_s, v_r, c_s, c_r, h_s, h_r) = scratch[10 + 3 * levels :]
    variants, samples = g.shape
    chunks = variants // CHUNK
    nb = probes_ref.shape[0]
    nv = nb + 1
    prow = psend.shape[1]
    rows = (nv + 1) * K
    half_rows = rows // 2
    total = samples * nsmp

    me_v = lax.axis_index("var")
    me_s = lax.axis_index("smp")
    core = me_v % 2

    def g_copy(i):
        part = pl.ds(i * CHUNK, CHUNK)
        return pltpu.make_async_copy(g_hbm.at[part], g.at[part], gsem.at[i])

    for i in range(chunks):
        g_copy(i).start()

    def smp_peer(o):
        return {"var": me_v, "smp": (me_s + o) % nsmp}

    def var_peer(bit):
        step = 1 << bit
        return {"var": me_v + step - 2 * step * ((me_v // step) % 2), "smp": me_s}

    barrier = pltpu.get_barrier_semaphore()
    for o in range(1, nsmp):
        pl.semaphore_signal(barrier, inc=1, device_id=smp_peer(o), device_id_type=MESH)
    for bit in range(levels + 1):
        pl.semaphore_signal(barrier, inc=1, device_id=var_peer(bit), device_id_type=MESH)

    row = lax.broadcasted_iota(jnp.int32, (vec.shape[0], samples), 0)
    lane = lax.broadcasted_iota(jnp.int32, (vec.shape[0], samples), 1)
    unit = (row == nv) | ((row == nv + 1) & (lane == 0))
    vec[...] = jnp.where(unit, 1.0, 0.0)
    vec[0:nb, :] = probes_ref[...].astype(jnp.float32)
    vec[nb : nb + 1, :] = phen_ref[...].astype(jnp.float32)
    vectors = vec[...].astype(jnp.bfloat16)
    vsum = jnp.sum(vec[0:prow, :], axis=1, keepdims=True)
    vsend[...] = jnp.broadcast_to(vsum, vsend.shape)
    ones = jnp.ones((16, 2 * LANES), jnp.bfloat16)

    def v_copy(o):
        return pltpu.make_async_remote_copy(
            src_ref=vsend, dst_ref=vrecv.at[o - 1], send_sem=v_s.at[o - 1],
            recv_sem=v_r.at[o - 1], device_id=smp_peer(o), device_id_type=MESH,
        )

    def p_copy(o, i):
        return pltpu.make_async_remote_copy(
            src_ref=psend.at[i], dst_ref=precv.at[o - 1, i], send_sem=p_s.at[o - 1, i],
            recv_sem=p_r.at[o - 1, i], device_id=smp_peer(o), device_id_type=MESH,
        )

    nt = (((1,), (1,)), ((), ()))
    for i in range(chunks):
        g_copy(i).wait()
        part = g[i * CHUNK : (i + 1) * CHUNK, :]
        prod = lax.dot_general(vectors, part, nt, preferred_element_type=jnp.float32)
        first = jnp.broadcast_to(part[:, 0:1].astype(jnp.float32), (CHUNK, LANES))
        acc = jnp.zeros((CHUNK, LANES), jnp.float32)
        for t in range(samples // LANES):
            d = part[:, t * LANES : (t + 1) * LANES].astype(jnp.float32) - first
            acc = acc + d * d
        hi = acc.astype(jnp.bfloat16)
        lo = (acc - hi.astype(jnp.float32)).astype(jnp.bfloat16)
        both = jnp.concatenate([hi, lo], axis=1)
        s2 = lax.dot_general(ones, both, nt, preferred_element_type=jnp.float32)[0:1, :]
        psend[i] = prod[0:prow, :]
        shifted = prod[nv : nv + 1, :] - samples * prod[nv + 1 : nv + 2, :]
        m2 = jnp.maximum(s2 - shifted * shifted / samples, 0.0)
        psend[i, nv + 1 : nv + 2, :] = m2
        if i == 0:
            pl.semaphore_wait(barrier, nsmp - 1 + levels + 1)
            for o in range(1, nsmp):
                v_copy(o).start()
        for o in range(1, nsmp):
            p_copy(o, i).start()

    corr[...] = jnp.zeros_like(corr)
    kind = lax.broadcasted_iota(jnp.int32, (K, CHUNK), 0)
    for o in range(1, nsmp):
        v_copy(o).wait()
    vtot = vsend[:, 0:1]
    for o in range(1, nsmp):
        vtot = vtot + vrecv[o - 1][:, 0:1]
    for i in range(chunks):
        cols = pl.ds(i * CHUNK, CHUNK)
        parts = [psend[i]]
        for o in range(1, nsmp):
            p_copy(o, i).wait()
            parts.append(precv[o - 1, i])
        psum = functools.reduce(lambda a, b: a + b, parts)
        mean = psum[nv : nv + 1, :] / total
        m2 = psum[nv + 1 : nv + 2, :]
        for p in parts:
            off = p[nv : nv + 1, :] / samples - mean
            m2 = m2 + samples * off * off
        inv = 1.0 / (m2 / total + EPS)
        a = (psum - mean * vtot) * inv
        member = lab_ref[:, cols] == kind
        mean8 = jnp.broadcast_to(mean, (K, CHUNK))
        for jj in range((nv + 1) // 2):
            pair = []
            for j in (2 * jj, 2 * jj + 1):
                if j < nv:
                    wj = jnp.where(member, jnp.broadcast_to(a[j : j + 1, :], (K, CHUNK)), 0.0)
                    wj = wj.astype(jnp.bfloat16).astype(jnp.float32)
                    cj = wj * mean8
                else:
                    wj = jnp.zeros((K, CHUNK), jnp.float32)
                    cj = jnp.where(member, -1.0, 0.0)
                pair.append(wj)
                fold = functools.reduce(
                    lambda x, y: x + y,
                    [cj[:, t * LANES : (t + 1) * LANES] for t in range(CHUNK // LANES)],
                )
                corr[j * K : (j + 1) * K, :] += fold
            w[2 * K * jj : 2 * K * (jj + 1), cols] = jnp.concatenate(pair, axis=0).astype(jnp.bfloat16)

    def c_copy(p):
        return pltpu.make_async_remote_copy(
            src_ref=buf.at[1 - core, p], dst_ref=crecv.at[p], send_sem=c_s.at[p],
            recv_sem=c_r.at[p], device_id=var_peer(0), device_id_type=MESH,
        )

    shift = jnp.sum(corr[...], axis=1, keepdims=True)
    low_lane = lax.broadcasted_iota(jnp.int32, (half_rows, LANES), 1) < LANES // 2
    weights = w[...]
    for c in range(samples // CHUNK):
        term = jnp.dot(weights, g[:, c * CHUNK : (c + 1) * CHUNK], preferred_element_type=jnp.float32)
        term = term - shift
        for u in range(CHUNK // LANES):
            t = c * (CHUNK // LANES) + u
            p = reverse_bits(t, levels)
            top = term[0:half_rows, u * LANES : (u + 1) * LANES]
            low = term[half_rows:rows, u * LANES : (u + 1) * LANES]
            buf[0, p] = jnp.where(low_lane, top, pltpu.roll(low, LANES // 2, 1))
            buf[1, p] = jnp.where(low_lane, pltpu.roll(top, LANES // 2, 1), low)
            c_copy(p).start()

    for p in range(tiles):
        c_copy(p).wait()
    left, right = buf.at[core], crecv
    count = tiles
    for level in range(levels):
        count //= 2
        bit = (me_v // (2 << level)) % 2
        away = pl.ds((1 - bit) * count, count)
        home = pl.ds(bit * count, count)
        copy = pltpu.make_async_remote_copy(
            src_ref=srcs[level], dst_ref=recvs[level], send_sem=h_s.at[level],
            recv_sem=h_r.at[level], device_id=var_peer(level + 1), device_id_type=MESH,
        )
        srcs[level][...] = left[away] + right[away]
        copy.start()
        keeps[level][...] = left[home] + right[home]
        copy.wait()
        left, right = keeps[level], recvs[level]
    res = left[0] + right[0]
    other = pltpu.roll(res, LANES // 2, 1)
    wide = LANES // 2
    counts = other[half_rows - K : half_rows, 0:wide]
    for j in range(nv):
        src = res if j * K < half_rows else other
        at = j * K % half_rows
        out_ref[:, j, :] = src[at : at + K, 0:wide] / counts


def solution(mesh):
    nvar, nsmp = mesh.shape["var"], mesh.shape["smp"]

    def body(genotype, labels, probes, phenotype):
        variants, samples = genotype.shape
        nv = probes.shape[0] + 1
        tiles = samples // LANES
        levels = tiles.bit_length() - 1
        chunks = variants // CHUNK
        prow = (nv + 2 + 7) // 8 * 8
        rows = (nv + 1) * K
        half = rows // 2
        f32 = jnp.float32
        halves = [pltpu.VMEM((tiles >> (level + 1), half, LANES), f32) for level in range(levels)]
        dma = pltpu.SemaphoreType.DMA
        out = pl.pallas_call(
            functools.partial(kernel, nsmp, nvar),
            out_shape=jax.ShapeDtypeStruct((K, nv, LANES // 2), f32),
            in_specs=[pl.BlockSpec(memory_space=pl.ANY)] + [pl.BlockSpec(memory_space=pltpu.VMEM)] * 3,
            out_specs=pl.BlockSpec(memory_space=pltpu.VMEM),
            scratch_shapes=[
                pltpu.VMEM((variants, samples), jnp.bfloat16),
                pltpu.VMEM((32, samples), f32),
                pltpu.VMEM((chunks, prow, CHUNK), f32),
                pltpu.VMEM((nsmp - 1, chunks, prow, CHUNK), f32),
                pltpu.VMEM((prow, LANES), f32),
                pltpu.VMEM((nsmp - 1, prow, LANES), f32),
                pltpu.VMEM((rows, variants), jnp.bfloat16),
                pltpu.VMEM((rows, LANES), f32),
                pltpu.VMEM((2, tiles, half, LANES), f32),
                pltpu.VMEM((tiles, half, LANES), f32),
                *halves, *halves, *halves,
                dma((chunks,)),
                dma((nsmp - 1, chunks)),
                dma((nsmp - 1, chunks)),
                dma((nsmp - 1,)),
                dma((nsmp - 1,)),
                dma((tiles,)),
                dma((tiles,)),
                dma((levels,)),
                dma((levels,)),
            ],
            compiler_params=pltpu.CompilerParams(
                collective_id=0, has_side_effects=True, vmem_limit_bytes=48 << 20
            ),
        )(genotype, labels.reshape(1, variants), probes, phenotype.reshape(1, samples))
        return out.reshape(K, nv, 1, LANES // 2)

    placed = (P("var", "smp"), P("var"), P(None, "smp"), P("smp"))
    return jax.shard_map(
        body, mesh=mesh, in_specs=placed, out_specs=P(None, None, "smp", "var"), check_vma=False
    )
```

```python
import functools

import jax
import jax.numpy as jnp
from jax import lax
from jax.experimental import pallas as pl
from jax.experimental.pallas import tpu as pltpu
from jax.sharding import PartitionSpec as P

K = 8
EPS = 1e-06
LANES = 128
CHUNK = 256
MESH = pl.DeviceIdType.MESH


def kernel(nsmp, nvar, g_hbm, lab_hbm, probes_hbm, phen_hbm, out_ref, *scratch):
    (g, lab_ref, probes_ref, phen_ref, vec, psend, precv, vsend, vrecv, w, corr, acc) = scratch[:12]
    (buf, crecv, ysend, ykeep, yrecv, zsend, zrecv) = scratch[12:19]
    (gsem, i_s, p_s, p_r, v_s, v_r, c_s, c_r, y_s, y_r, z_s, z_r) = scratch[19:]
    variants, samples = g.shape
    chunks = variants // CHUNK
    nz = nvar // 4
    nb = probes_ref.shape[0]
    nv = nb + 1
    prow = psend.shape[1]
    rows = (nv + 1) * K
    half_rows = rows // 2
    total = samples * nsmp

    me_v = lax.axis_index("var")
    me_s = lax.axis_index("smp")
    core = me_v % 2
    why = (me_v // 2) % 2
    zed = me_v // 4

    def g_copy(i):
        part = pl.ds(i * CHUNK, CHUNK)
        return pltpu.make_async_copy(g_hbm.at[part], g.at[part], gsem.at[i])

    small = [
        pltpu.make_async_copy(probes_hbm, probes_ref, i_s.at[0]),
        pltpu.make_async_copy(phen_hbm, phen_ref, i_s.at[1]),
        pltpu.make_async_copy(lab_hbm, lab_ref, i_s.at[2]),
    ]
    for copy in small[:2]:
        copy.start()
    for i in range(chunks):
        g_copy(i).start()
    small[2].start()

    def smp_peer(o):
        return {"var": me_v, "smp": (me_s + o) % nsmp}

    def var_peer(offset):
        at = 0
        for bit in range(nvar.bit_length() - 1):
            step = 1 << bit
            at = at + step * (((me_v // step) + (offset // step)) % 2)
        return {"var": at, "smp": me_s}

    def zed_xor(offset):
        at = 0
        for bit in range(nz.bit_length() - 1):
            step = 1 << bit
            at = at + step * (((zed // step) + (offset // step)) % 2)
        return at

    barrier = pltpu.get_barrier_semaphore()
    for o in range(1, nsmp):
        pl.semaphore_signal(barrier, inc=1, device_id=smp_peer(o), device_id_type=MESH)
    partners = [1, 2] + [4 * o for o in range(1, nz)]
    for offset in partners:
        pl.semaphore_signal(barrier, inc=1, device_id=var_peer(offset), device_id_type=MESH)

    row = lax.broadcasted_iota(jnp.int32, (vec.shape[0], samples), 0)
    lane = lax.broadcasted_iota(jnp.int32, (vec.shape[0], samples), 1)
    unit = (row == nv) | ((row == nv + 1) & (lane == 0))
    vec[...] = jnp.where(unit, 1.0, 0.0)
    small[0].wait()
    small[1].wait()
    vec[0:nb, :] = probes_ref[...].astype(jnp.float32)
    phen = phen_ref[...].astype(jnp.float32)
    for t in range(samples // LANES):
        vec[nb : nb + 1, t * LANES : (t + 1) * LANES] = phen[t : t + 1, :]
    vectors = vec[...].astype(jnp.bfloat16)
    vsum = jnp.sum(vec[0:prow, :], axis=1, keepdims=True)
    vsend[...] = jnp.broadcast_to(vsum, vsend.shape)
    ones = jnp.ones((16, 2 * LANES), jnp.bfloat16)

    def v_copy(o):
        return pltpu.make_async_remote_copy(
            src_ref=vsend, dst_ref=vrecv.at[o - 1], send_sem=v_s.at[o - 1],
            recv_sem=v_r.at[o - 1], device_id=smp_peer(o), device_id_type=MESH,
        )

    def p_copy(o, i):
        return pltpu.make_async_remote_copy(
            src_ref=psend.at[i], dst_ref=precv.at[o - 1, i], send_sem=p_s.at[o - 1, i],
            recv_sem=p_r.at[o - 1, i], device_id=smp_peer(o), device_id_type=MESH,
        )

    nt = (((1,), (1,)), ((), ()))
    for i in range(chunks):
        g_copy(i).wait()
        part = g[i * CHUNK : (i + 1) * CHUNK, :]
        prod = lax.dot_general(vectors, part, nt, preferred_element_type=jnp.float32)
        first = jnp.broadcast_to(part[:, 0:1].astype(jnp.float32), (CHUNK, LANES))
        square = jnp.zeros((CHUNK, LANES), jnp.float32)
        for t in range(samples // LANES):
            d = part[:, t * LANES : (t + 1) * LANES].astype(jnp.float32) - first
            square = square + d * d
        hi = square.astype(jnp.bfloat16)
        lo = (square - hi.astype(jnp.float32)).astype(jnp.bfloat16)
        both = jnp.concatenate([hi, lo], axis=1)
        s2 = lax.dot_general(ones, both, nt, preferred_element_type=jnp.float32)[0:1, :]
        psend[i] = prod[0:prow, :]
        shifted = prod[nv : nv + 1, :] - samples * prod[nv + 1 : nv + 2, :]
        m2 = jnp.maximum(s2 - shifted * shifted / samples, 0.0)
        psend[i, nv + 1 : nv + 2, :] = m2
        if i == 0:
            pl.semaphore_wait(barrier, nsmp - 1 + len(partners))
            for o in range(1, nsmp):
                v_copy(o).start()
        for o in range(1, nsmp):
            p_copy(o, i).start()

    corr[...] = jnp.zeros_like(corr)
    small[2].wait()
    kind = lax.broadcasted_iota(jnp.int32, (K, CHUNK), 0)
    for o in range(1, nsmp):
        v_copy(o).wait()
    vtot = vsend[:, 0:1]
    for o in range(1, nsmp):
        vtot = vtot + vrecv[o - 1][:, 0:1]

    def weigh(i):
        cols = pl.ds(i * CHUNK, CHUNK)
        parts = [psend[i]]
        for o in range(1, nsmp):
            p_copy(o, i).wait()
            parts.append(precv[o - 1, i])
        psum = functools.reduce(lambda a, b: a + b, parts)
        mean = psum[nv : nv + 1, :] / total
        m2 = psum[nv + 1 : nv + 2, :]
        for p in parts:
            off = p[nv : nv + 1, :] / samples - mean
            m2 = m2 + samples * off * off
        inv = 1.0 / (m2 / total + EPS)
        a = (psum - mean * vtot) * inv
        member = lab_ref[:, cols] == kind
        mean8 = jnp.broadcast_to(mean, (K, CHUNK))
        for jj in range((nv + 1) // 2):
            pair = []
            for j in (2 * jj, 2 * jj + 1):
                if j < nv:
                    wj = jnp.where(member, jnp.broadcast_to(a[j : j + 1, :], (K, CHUNK)), 0.0)
                    wj = wj.astype(jnp.bfloat16).astype(jnp.float32)
                    cj = wj * mean8
                else:
                    wj = jnp.zeros((K, CHUNK), jnp.float32)
                    cj = jnp.where(member, -1.0, 0.0)
                pair.append(wj)
                fold = functools.reduce(
                    lambda x, y: x + y,
                    [cj[:, t * LANES : (t + 1) * LANES] for t in range(CHUNK // LANES)],
                )
                corr[j * K : (j + 1) * K, :] += fold
            w[2 * K * jj : 2 * K * (jj + 1), cols] = jnp.concatenate(pair, axis=0).astype(jnp.bfloat16)

    early = chunks * 3 // 4
    for i in range(early):
        weigh(i)
    cut = early * CHUNK
    width = 2 * LANES
    for c in range(nz):
        cols = slice(c * width, (c + 1) * width)
        acc[:, cols] = jnp.dot(w[:, 0:cut], g[0:cut, cols], preferred_element_type=jnp.float32)
    for i in range(early, chunks):
        weigh(i)

    def c_copy(u):
        return pltpu.make_async_remote_copy(
            src_ref=buf.at[1 - core, u], dst_ref=crecv.at[u], send_sem=c_s.at[u],
            recv_sem=c_r.at[u], device_id=var_peer(1), device_id_type=MESH,
        )

    def y_copy(u):
        return pltpu.make_async_remote_copy(
            src_ref=ysend.at[u], dst_ref=yrecv.at[u], send_sem=y_s.at[u],
            recv_sem=y_r.at[u], device_id=var_peer(2), device_id_type=MESH,
        )

    def z_copy(u):
        return pltpu.make_async_remote_copy(
            src_ref=zsend.at[u], dst_ref=zrecv.at[u], send_sem=z_s.at[u],
            recv_sem=z_r.at[u], device_id=var_peer(4 * (nz - 1 - u)), device_id_type=MESH,
        )

    shift = jnp.sum(corr[...], axis=1, keepdims=True)
    low_lane = lax.broadcasted_iota(jnp.int32, (half_rows, LANES), 1) < LANES // 2
    tail = w[:, cut:variants]

    def step_c(u):
        cols = pl.ds(pl.multiple_of(zed_xor(nz - 1 - u) * width, width), width)
        term = acc[:, cols] + jnp.dot(tail, g[cut:variants, cols], preferred_element_type=jnp.float32)
        term = term - shift
        for t in range(2):
            top = term[0:half_rows, t * LANES : (t + 1) * LANES]
            low = term[half_rows:rows, t * LANES : (t + 1) * LANES]
            buf[0, u, t] = jnp.where(low_lane, top, pltpu.roll(low, LANES // 2, 1))
            buf[1, u, t] = jnp.where(low_lane, pltpu.roll(top, LANES // 2, 1), low)
        c_copy(u).start()

    def step_y(u):
        c_copy(u).wait()
        ysend[u] = buf[core, u, 1 - why] + crecv[u, 1 - why]
        y_copy(u).start()
        ykeep[u] = buf[core, u, why] + crecv[u, why]

    def step_z(u):
        y_copy(u).wait()
        zsend[u] = ykeep[u] + yrecv[u]
        if u < nz - 1:
            z_copy(u).start()

    for s in range(nz + 3):
        if s < nz:
            step_c(s)
        if 0 <= s - 1 < nz:
            step_y(s - 1)
        if 0 <= s - 3 < nz:
            step_z(s - 3)

    res = zsend[nz - 1]
    for u in range(nz - 2, -1, -1):
        z_copy(u).wait()
        res = res + zrecv[u]
    other = pltpu.roll(res, LANES // 2, 1)
    wide = LANES // 2
    counts = other[half_rows - K : half_rows, 0:wide]
    for j in range(nv):
        src = res if j * K < half_rows else other
        at = j * K % half_rows
        out_ref[:, j, :] = src[at : at + K, 0:wide] / counts


def solution(mesh):
    nvar, nsmp = mesh.shape["var"], mesh.shape["smp"]

    def body(genotype, labels, probes, phenotype):
        variants, samples = genotype.shape
        nb = probes.shape[0]
        nv = nb + 1
        nz = nvar // 4
        chunks = variants // CHUNK
        prow = (nv + 2 + 7) // 8 * 8
        rows = (nv + 1) * K
        half = rows // 2
        f32 = jnp.float32
        dma = pltpu.SemaphoreType.DMA
        out = pl.pallas_call(
            functools.partial(kernel, nsmp, nvar),
            out_shape=jax.ShapeDtypeStruct((K, nv, LANES // 2), f32),
            in_specs=[pl.BlockSpec(memory_space=pltpu.MemorySpace.HBM)] * 4,
            out_specs=pl.BlockSpec(memory_space=pltpu.VMEM),
            scratch_shapes=[
                pltpu.VMEM((variants, samples), jnp.bfloat16),
                pltpu.VMEM((1, variants), jnp.int32),
                pltpu.VMEM((nb, samples), jnp.bfloat16),
                pltpu.VMEM((samples // LANES, LANES), jnp.bfloat16),
                pltpu.VMEM((32, samples), f32),
                pltpu.VMEM((chunks, prow, CHUNK), f32),
                pltpu.VMEM((nsmp - 1, chunks, prow, CHUNK), f32),
                pltpu.VMEM((prow, LANES), f32),
                pltpu.VMEM((nsmp - 1, prow, LANES), f32),
                pltpu.VMEM((rows, variants), jnp.bfloat16),
                pltpu.VMEM((rows, LANES), f32),
                pltpu.VMEM((rows, samples), f32),
                pltpu.VMEM((2, nz, 2, half, LANES), f32),
                pltpu.VMEM((nz, 2, half, LANES), f32),
                pltpu.VMEM((nz, half, LANES), f32),
                pltpu.VMEM((nz, half, LANES), f32),
                pltpu.VMEM((nz, half, LANES), f32),
                pltpu.VMEM((nz, half, LANES), f32),
                pltpu.VMEM((nz - 1, half, LANES), f32),
                dma((chunks,)),
                dma((3,)),
                dma((nsmp - 1, chunks)),
                dma((nsmp - 1, chunks)),
                dma((nsmp - 1,)),
                dma((nsmp - 1,)),
                dma((nz,)),
                dma((nz,)),
                dma((nz,)),
                dma((nz,)),
                dma((nz - 1,)),
                dma((nz - 1,)),
            ],
            compiler_params=pltpu.CompilerParams(
                collective_id=0, has_side_effects=True, vmem_limit_bytes=67043328
            ),
        )(genotype, labels.reshape(1, variants), probes, phenotype.reshape(samples // LANES, LANES))
        return out.reshape(K, nv, 1, LANES // 2)

    placed = (P("var", "smp"), P("var"), P(None, "smp"), P("smp"))
    return jax.shard_map(
        body, mesh=mesh, in_specs=placed, out_specs=P(None, None, "smp", "var"), check_vma=False
    )
```

```python
import functools

import jax
import jax.numpy as jnp
from jax import lax
from jax.experimental import pallas as pl
from jax.experimental.pallas import tpu as pltpu
from jax.sharding import PartitionSpec as P

K = 8
EPS = 1e-06
LANES = 128
CHUNK = 256
MESH = pl.DeviceIdType.MESH


def kernel(nsmp, nvar, g_hbm, lab_hbm, probes_hbm, phen_hbm, out_ref, *scratch):
    (g, lab_ref, probes_ref, phen_ref, vec, psend, precv, vsend, vrecv, w, corr, acc) = scratch[:12]
    (buf, crecv, ysend, ykeep, yrecv, zsend, zrecv) = scratch[12:19]
    (gsem, i_s, p_s, p_r, v_s, v_r, c_s, c_r, y_s, y_r, z_s, z_r, word) = scratch[19:]
    variants, samples = g.shape
    chunks = variants // CHUNK
    nz = nvar // 4
    nb = probes_ref.shape[0]
    nv = nb + 1
    prow = psend.shape[1]
    rows = (nv + 1) * K
    half_rows = rows // 2
    total = samples * nsmp

    me_v = lax.axis_index("var")
    me_s = lax.axis_index("smp")
    core = me_v % 2
    why = (me_v // 2) % 2
    zed = me_v // 4

    def g_copy(i):
        part = pl.ds(i * CHUNK, CHUNK)
        return pltpu.make_async_copy(g_hbm.at[part], g.at[part], gsem.at[i])

    small = [
        pltpu.make_async_copy(probes_hbm, probes_ref, i_s.at[0]),
        pltpu.make_async_copy(phen_hbm, phen_ref, i_s.at[1]),
        pltpu.make_async_copy(lab_hbm, lab_ref, i_s.at[2]),
    ]
    for copy in small[:2]:
        copy.start()
    for i in range(chunks):
        g_copy(i).start()
    small[2].start()

    def smp_peer(o):
        return {"var": me_v, "smp": (me_s + o) % nsmp}

    def var_peer(offset):
        at = 0
        for bit in range(nvar.bit_length() - 1):
            step = 1 << bit
            at = at + step * (((me_v // step) + (offset // step)) % 2)
        return {"var": at, "smp": me_s}

    def zed_xor(offset):
        at = 0
        for bit in range(nz.bit_length() - 1):
            step = 1 << bit
            at = at + step * (((zed // step) + (offset // step)) % 2)
        return at

    barrier = pltpu.get_barrier_semaphore()
    for o in range(1, nsmp):
        pl.semaphore_signal(barrier, inc=1, device_id=smp_peer(o), device_id_type=MESH)
    for offset in (1, 2):
        pl.semaphore_signal(barrier, inc=1, device_id=var_peer(offset), device_id_type=MESH)
    beside = jnp.where(zed > 0, 1, 0) + jnp.where(zed < nz - 1, 1, 0)

    def tell(sem):
        @pl.when(zed > 0)
        def _():
            pl.semaphore_signal(
                sem, inc=1, device_id={"var": me_v - 4, "smp": me_s}, device_id_type=MESH
            )

        @pl.when(zed < nz - 1)
        def _():
            pl.semaphore_signal(
                sem, inc=1, device_id={"var": me_v + 4, "smp": me_s}, device_id_type=MESH
            )

    def hear(r):
        if r < nz - 2:
            pl.semaphore_wait(word.at[r], beside)
            if r + 1 < nz - 2:
                tell(word.at[r + 1])

    tell(barrier)

    row = lax.broadcasted_iota(jnp.int32, (vec.shape[0], samples), 0)
    lane = lax.broadcasted_iota(jnp.int32, (vec.shape[0], samples), 1)
    unit = (row == nv) | ((row == nv + 1) & (lane == 0))
    vec[...] = jnp.where(unit, 1.0, 0.0)
    small[0].wait()
    small[1].wait()
    vec[0:nb, :] = probes_ref[...].astype(jnp.float32)
    phen = phen_ref[...].astype(jnp.float32)
    for t in range(samples // LANES):
        vec[nb : nb + 1, t * LANES : (t + 1) * LANES] = phen[t : t + 1, :]
    vectors = vec[...].astype(jnp.bfloat16)
    vsum = jnp.sum(vec[0:prow, :], axis=1, keepdims=True)
    vsend[...] = jnp.broadcast_to(vsum, vsend.shape)
    ones = jnp.ones((16, 2 * LANES), jnp.bfloat16)

    def v_copy(o):
        return pltpu.make_async_remote_copy(
            src_ref=vsend, dst_ref=vrecv.at[o - 1], send_sem=v_s.at[o - 1],
            recv_sem=v_r.at[o - 1], device_id=smp_peer(o), device_id_type=MESH,
        )

    def p_copy(o, i):
        return pltpu.make_async_remote_copy(
            src_ref=psend.at[i], dst_ref=precv.at[o - 1, i], send_sem=p_s.at[o - 1, i],
            recv_sem=p_r.at[o - 1, i], device_id=smp_peer(o), device_id_type=MESH,
        )

    nt = (((1,), (1,)), ((), ()))
    for i in range(chunks):
        g_copy(i).wait()
        part = g[i * CHUNK : (i + 1) * CHUNK, :]
        prod = lax.dot_general(vectors, part, nt, preferred_element_type=jnp.float32)
        first = jnp.broadcast_to(part[:, 0:1].astype(jnp.float32), (CHUNK, LANES))
        square = jnp.zeros((CHUNK, LANES), jnp.float32)
        for t in range(samples // LANES):
            d = part[:, t * LANES : (t + 1) * LANES].astype(jnp.float32) - first
            square = square + d * d
        hi = square.astype(jnp.bfloat16)
        lo = (square - hi.astype(jnp.float32)).astype(jnp.bfloat16)
        both = jnp.concatenate([hi, lo], axis=1)
        s2 = lax.dot_general(ones, both, nt, preferred_element_type=jnp.float32)[0:1, :]
        psend[i] = prod[0:prow, :]
        shifted = prod[nv : nv + 1, :] - samples * prod[nv + 1 : nv + 2, :]
        m2 = jnp.maximum(s2 - shifted * shifted / samples, 0.0)
        psend[i, nv + 1 : nv + 2, :] = m2
        if i == 0:
            pl.semaphore_wait(barrier, nsmp - 1 + 2 + beside)
            if nz > 2:
                tell(word.at[0])
            for o in range(1, nsmp):
                v_copy(o).start()
        for o in range(1, nsmp):
            p_copy(o, i).start()

    corr[...] = jnp.zeros_like(corr)
    small[2].wait()
    for r in range(nz - 2):
        hear(r)
    kind = lax.broadcasted_iota(jnp.int32, (K, CHUNK), 0)
    for o in range(1, nsmp):
        v_copy(o).wait()
    vtot = vsend[:, 0:1]
    for o in range(1, nsmp):
        vtot = vtot + vrecv[o - 1][:, 0:1]

    def weigh(i):
        cols = pl.ds(i * CHUNK, CHUNK)
        parts = [psend[i]]
        for o in range(1, nsmp):
            p_copy(o, i).wait()
            parts.append(precv[o - 1, i])
        psum = functools.reduce(lambda a, b: a + b, parts)
        mean = psum[nv : nv + 1, :] / total
        m2 = psum[nv + 1 : nv + 2, :]
        for p in parts:
            off = p[nv : nv + 1, :] / samples - mean
            m2 = m2 + samples * off * off
        inv = 1.0 / (m2 / total + EPS)
        a = (psum - mean * vtot) * inv
        member = lab_ref[:, cols] == kind
        mean8 = jnp.broadcast_to(mean, (K, CHUNK))
        for jj in range((nv + 1) // 2):
            pair = []
            for j in (2 * jj, 2 * jj + 1):
                if j < nv:
                    wj = jnp.where(member, jnp.broadcast_to(a[j : j + 1, :], (K, CHUNK)), 0.0)
                    wj = wj.astype(jnp.bfloat16).astype(jnp.float32)
                    cj = wj * mean8
                else:
                    wj = jnp.zeros((K, CHUNK), jnp.float32)
                    cj = jnp.where(member, -1.0, 0.0)
                pair.append(wj)
                fold = functools.reduce(
                    lambda x, y: x + y,
                    [cj[:, t * LANES : (t + 1) * LANES] for t in range(CHUNK // LANES)],
                )
                corr[j * K : (j + 1) * K, :] += fold
            w[2 * K * jj : 2 * K * (jj + 1), cols] = jnp.concatenate(pair, axis=0).astype(jnp.bfloat16)

    early = chunks * 3 // 4
    for i in range(early):
        weigh(i)
    cut = early * CHUNK
    width = 2 * LANES
    for c in range(nz):
        cols = slice(c * width, (c + 1) * width)
        acc[:, cols] = jnp.dot(w[:, 0:cut], g[0:cut, cols], preferred_element_type=jnp.float32)
    for i in range(early, chunks):
        weigh(i)

    def c_copy(u):
        return pltpu.make_async_remote_copy(
            src_ref=buf.at[1 - core, u], dst_ref=crecv.at[u], send_sem=c_s.at[u],
            recv_sem=c_r.at[u], device_id=var_peer(1), device_id_type=MESH,
        )

    def y_copy(u):
        return pltpu.make_async_remote_copy(
            src_ref=ysend.at[u], dst_ref=yrecv.at[u], send_sem=y_s.at[u],
            recv_sem=y_r.at[u], device_id=var_peer(2), device_id_type=MESH,
        )

    def z_copy(u):
        return pltpu.make_async_remote_copy(
            src_ref=zsend.at[u], dst_ref=zrecv.at[u], send_sem=z_s.at[u],
            recv_sem=z_r.at[u], device_id=var_peer(4 * (nz - 1 - u)), device_id_type=MESH,
        )

    shift = jnp.sum(corr[...], axis=1, keepdims=True)
    low_lane = lax.broadcasted_iota(jnp.int32, (half_rows, LANES), 1) < LANES // 2
    tail = w[:, cut:variants]

    def step_c(u):
        cols = pl.ds(pl.multiple_of(zed_xor(nz - 1 - u) * width, width), width)
        term = acc[:, cols] + jnp.dot(tail, g[cut:variants, cols], preferred_element_type=jnp.float32)
        term = term - shift
        for t in range(2):
            top = term[0:half_rows, t * LANES : (t + 1) * LANES]
            low = term[half_rows:rows, t * LANES : (t + 1) * LANES]
            buf[0, u, t] = jnp.where(low_lane, top, pltpu.roll(low, LANES // 2, 1))
            buf[1, u, t] = jnp.where(low_lane, pltpu.roll(top, LANES // 2, 1), low)
        c_copy(u).start()

    def step_y(u):
        c_copy(u).wait()
        ysend[u] = buf[core, u, 1 - why] + crecv[u, 1 - why]
        y_copy(u).start()
        ykeep[u] = buf[core, u, why] + crecv[u, why]

    def step_z(u):
        y_copy(u).wait()
        zsend[u] = ykeep[u] + yrecv[u]
        if u < nz - 1:
            z_copy(u).start()

    for s in range(nz + 3):
        if s < nz:
            step_c(s)
        if 0 <= s - 1 < nz:
            step_y(s - 1)
        if 0 <= s - 3 < nz:
            step_z(s - 3)

    res = zsend[nz - 1]
    for u in range(nz - 2, -1, -1):
        z_copy(u).wait()
        res = res + zrecv[u]
    other = pltpu.roll(res, LANES // 2, 1)
    wide = LANES // 2
    counts = other[half_rows - K : half_rows, 0:wide]
    for j in range(nv):
        src = res if j * K < half_rows else other
        at = j * K % half_rows
        out_ref[:, j, :] = src[at : at + K, 0:wide] / counts


def solution(mesh):
    nvar, nsmp = mesh.shape["var"], mesh.shape["smp"]

    def body(genotype, labels, probes, phenotype):
        variants, samples = genotype.shape
        nb = probes.shape[0]
        nv = nb + 1
        nz = nvar // 4
        chunks = variants // CHUNK
        prow = (nv + 2 + 7) // 8 * 8
        rows = (nv + 1) * K
        half = rows // 2
        f32 = jnp.float32
        dma = pltpu.SemaphoreType.DMA
        out = pl.pallas_call(
            functools.partial(kernel, nsmp, nvar),
            out_shape=jax.ShapeDtypeStruct((K, nv, LANES // 2), f32),
            in_specs=[pl.BlockSpec(memory_space=pltpu.MemorySpace.HBM)] * 4,
            out_specs=pl.BlockSpec(memory_space=pltpu.VMEM),
            scratch_shapes=[
                pltpu.VMEM((variants, samples), jnp.bfloat16),
                pltpu.VMEM((1, variants), jnp.int32),
                pltpu.VMEM((nb, samples), jnp.bfloat16),
                pltpu.VMEM((samples // LANES, LANES), jnp.bfloat16),
                pltpu.VMEM((32, samples), f32),
                pltpu.VMEM((chunks, prow, CHUNK), f32),
                pltpu.VMEM((nsmp - 1, chunks, prow, CHUNK), f32),
                pltpu.VMEM((prow, LANES), f32),
                pltpu.VMEM((nsmp - 1, prow, LANES), f32),
                pltpu.VMEM((rows, variants), jnp.bfloat16),
                pltpu.VMEM((rows, LANES), f32),
                pltpu.VMEM((rows, samples), f32),
                pltpu.VMEM((2, nz, 2, half, LANES), f32),
                pltpu.VMEM((nz, 2, half, LANES), f32),
                pltpu.VMEM((nz, half, LANES), f32),
                pltpu.VMEM((nz, half, LANES), f32),
                pltpu.VMEM((nz, half, LANES), f32),
                pltpu.VMEM((nz, half, LANES), f32),
                pltpu.VMEM((nz - 1, half, LANES), f32),
                dma((chunks,)),
                dma((3,)),
                dma((nsmp - 1, chunks)),
                dma((nsmp - 1, chunks)),
                dma((nsmp - 1,)),
                dma((nsmp - 1,)),
                dma((nz,)),
                dma((nz,)),
                dma((nz,)),
                dma((nz,)),
                dma((nz - 1,)),
                dma((nz - 1,)),
                pltpu.SemaphoreType.REGULAR((max(nz - 2, 1),)),
            ],
            compiler_params=pltpu.CompilerParams(
                collective_id=0, has_side_effects=True, vmem_limit_bytes=48 << 20
            ),
        )(
            *[
                pltpu.with_memory_space_constraint(x, pltpu.HBM)
                for x in (
                    genotype,
                    labels.reshape(1, variants),
                    probes,
                    phenotype.reshape(samples // LANES, LANES),
                )
            ]
        )
        return out.reshape(K, nv, 1, LANES // 2)

    placed = (P("var", "smp"), P("var"), P(None, "smp"), P("smp"))
    return jax.shard_map(
        body, mesh=mesh, in_specs=placed, out_specs=P(None, None, "smp", "var"), check_vma=False
    )
```

```python
import functools

import jax
import jax.numpy as jnp
from jax import lax
from jax.experimental import pallas as pl
from jax.experimental.pallas import tpu as pltpu
from jax.sharding import PartitionSpec as P

K = 8
EPS = 1e-06
LANES = 128
CHUNK = 512
SPLIT = 24
MESH = pl.DeviceIdType.MESH


def kernel(nsmp, nvar, g_hbm, lab_hbm, probes_hbm, phen_hbm, out_ref, *scratch):
    (g, lab_ref, probes_ref, phen_ref, vec, psend, precv, vsend, vrecv, w, corr, acc) = scratch[:12]
    (buf, crecv, ysend, ykeep, yrecv, zsend, zrecv, asend, arecv, bsend, brecv) = scratch[12:23]
    (gsem, i_s, p_s, p_r, v_s, v_r, c_s, c_r, y_s, y_r, z_s, z_r, a_s, a_r, b_s, b_r, word) = scratch[23:]
    variants, samples = g.shape
    chunks = variants // CHUNK
    nz = nvar // 4
    nb = probes_ref.shape[0]
    nv = nb + 1
    prow = psend.shape[1]
    rows = (nv + 1) * K
    half_rows = rows // 2
    total = samples * nsmp

    me_v = lax.axis_index("var")
    me_s = lax.axis_index("smp")
    core = me_v % 2
    why = (me_v // 2) % 2
    zed = me_v // 4

    def g_copy(i):
        part = pl.ds(i * CHUNK, CHUNK)
        return pltpu.make_async_copy(g_hbm.at[part], g.at[part], gsem.at[i])

    small = [
        pltpu.make_async_copy(probes_hbm, probes_ref, i_s.at[0]),
        pltpu.make_async_copy(phen_hbm, phen_ref, i_s.at[1]),
        pltpu.make_async_copy(lab_hbm, lab_ref, i_s.at[2]),
    ]
    for copy in small[:2]:
        copy.start()
    for i in range(chunks):
        g_copy(i).start()
    small[2].start()

    def smp_peer(o):
        return {"var": me_v, "smp": (me_s + o) % nsmp}

    def var_peer(offset):
        at = 0
        for bit in range(nvar.bit_length() - 1):
            step = 1 << bit
            at = at + step * (((me_v // step) + (offset // step)) % 2)
        return {"var": at, "smp": me_s}

    def zed_xor(offset):
        at = 0
        for bit in range(nz.bit_length() - 1):
            step = 1 << bit
            at = at + step * (((zed // step) + (offset // step)) % 2)
        return at

    barrier = pltpu.get_barrier_semaphore()
    for o in range(1, nsmp):
        pl.semaphore_signal(barrier, inc=1, device_id=smp_peer(o), device_id_type=MESH)
    for offset in (1, 2):
        pl.semaphore_signal(barrier, inc=1, device_id=var_peer(offset), device_id_type=MESH)
    beside = jnp.where(zed > 0, 1, 0) + jnp.where(zed < nz - 1, 1, 0)

    def tell(sem):
        @pl.when(zed > 0)
        def _():
            pl.semaphore_signal(
                sem, inc=1, device_id={"var": me_v - 4, "smp": me_s}, device_id_type=MESH
            )

        @pl.when(zed < nz - 1)
        def _():
            pl.semaphore_signal(
                sem, inc=1, device_id={"var": me_v + 4, "smp": me_s}, device_id_type=MESH
            )

    def hear(r):
        if r < nz - 2:
            pl.semaphore_wait(word.at[r], beside)
            if r + 1 < nz - 2:
                tell(word.at[r + 1])

    tell(barrier)

    row = lax.broadcasted_iota(jnp.int32, (vec.shape[0], samples), 0)
    lane = lax.broadcasted_iota(jnp.int32, (vec.shape[0], samples), 1)
    unit = (row == nv) | ((row == nv + 1) & (lane == 0))
    vec[...] = jnp.where(unit, 1.0, 0.0)
    small[0].wait()
    small[1].wait()
    vec[0:nb, :] = probes_ref[...].astype(jnp.float32)
    phen = phen_ref[...].astype(jnp.float32)
    for t in range(samples // LANES):
        vec[nb : nb + 1, t * LANES : (t + 1) * LANES] = phen[t : t + 1, :]
    vectors = vec[...].astype(jnp.bfloat16)
    vsum = jnp.sum(vec[0:prow, :], axis=1, keepdims=True)
    vsend[...] = jnp.broadcast_to(vsum, vsend.shape)
    ones = jnp.ones((16, 2 * LANES), jnp.bfloat16)

    def v_copy(o):
        return pltpu.make_async_remote_copy(
            src_ref=vsend, dst_ref=vrecv.at[o - 1], send_sem=v_s.at[o - 1],
            recv_sem=v_r.at[o - 1], device_id=smp_peer(o), device_id_type=MESH,
        )

    def p_copy(o, i):
        return pltpu.make_async_remote_copy(
            src_ref=psend.at[i], dst_ref=precv.at[o - 1, i], send_sem=p_s.at[o - 1, i],
            recv_sem=p_r.at[o - 1, i], device_id=smp_peer(o), device_id_type=MESH,
        )

    nt = (((1,), (1,)), ((), ()))
    for i in range(chunks):
        g_copy(i).wait()
        part = g[i * CHUNK : (i + 1) * CHUNK, :]
        prod = lax.dot_general(vectors, part, nt, preferred_element_type=jnp.float32)
        first = jnp.broadcast_to(part[:, 0:1].astype(jnp.float32), (CHUNK, LANES))
        square = jnp.zeros((CHUNK, LANES), jnp.float32)
        for t in range(samples // LANES):
            d = part[:, t * LANES : (t + 1) * LANES].astype(jnp.float32) - first
            square = square + d * d
        hi = square.astype(jnp.bfloat16)
        lo = (square - hi.astype(jnp.float32)).astype(jnp.bfloat16)
        both = jnp.concatenate([hi, lo], axis=1)
        s2 = lax.dot_general(ones, both, nt, preferred_element_type=jnp.float32)[0:1, :]
        psend[i] = prod[0:prow, :]
        shifted = prod[nv : nv + 1, :] - samples * prod[nv + 1 : nv + 2, :]
        m2 = jnp.maximum(s2 - shifted * shifted / samples, 0.0)
        psend[i, nv + 1 : nv + 2, :] = m2
        if i == 0:
            pl.semaphore_wait(barrier, nsmp - 1 + 2 + beside)
            if nz > 2:
                tell(word.at[0])
            for o in range(1, nsmp):
                v_copy(o).start()
        for o in range(1, nsmp):
            p_copy(o, i).start()

    corr[...] = jnp.zeros_like(corr)
    small[2].wait()
    for r in range(nz - 2):
        hear(r)
    kind = lax.broadcasted_iota(jnp.int32, (K, CHUNK), 0)
    for o in range(1, nsmp):
        v_copy(o).wait()
    vtot = vsend[:, 0:1]
    for o in range(1, nsmp):
        vtot = vtot + vrecv[o - 1][:, 0:1]

    def weigh(i):
        cols = pl.ds(i * CHUNK, CHUNK)
        parts = [psend[i]]
        for o in range(1, nsmp):
            p_copy(o, i).wait()
            parts.append(precv[o - 1, i])
        psum = functools.reduce(lambda a, b: a + b, parts)
        mean = psum[nv : nv + 1, :] / total
        m2 = psum[nv + 1 : nv + 2, :]
        for p in parts:
            off = p[nv : nv + 1, :] / samples - mean
            m2 = m2 + samples * off * off
        inv = 1.0 / (m2 / total + EPS)
        a = (psum - mean * vtot) * inv
        member = lab_ref[:, cols] == kind
        mean8 = jnp.broadcast_to(mean, (K, CHUNK))
        for jj in range((nv + 1) // 2):
            pair = []
            for j in (2 * jj, 2 * jj + 1):
                if j < nv:
                    wj = jnp.where(member, jnp.broadcast_to(a[j : j + 1, :], (K, CHUNK)), 0.0)
                    wj = wj.astype(jnp.bfloat16).astype(jnp.float32)
                    cj = wj * mean8
                else:
                    wj = jnp.zeros((K, CHUNK), jnp.float32)
                    cj = jnp.where(member, -1.0, 0.0)
                pair.append(wj)
                fold = functools.reduce(
                    lambda x, y: x + y,
                    [cj[:, t * LANES : (t + 1) * LANES] for t in range(CHUNK // LANES)],
                )
                corr[j * K : (j + 1) * K, :] += fold
            w[2 * K * jj : 2 * K * (jj + 1), cols] = jnp.concatenate(pair, axis=0).astype(jnp.bfloat16)

    early = chunks // 2
    for i in range(early):
        weigh(i)
    cut = early * CHUNK
    width = 2 * LANES
    for c in range(nz):
        cols = slice(c * width, (c + 1) * width)
        acc[:, cols] = jnp.dot(w[:, 0:cut], g[0:cut, cols], preferred_element_type=jnp.float32)
    for i in range(early, chunks):
        weigh(i)

    def c_copy(u):
        return pltpu.make_async_remote_copy(
            src_ref=buf.at[1 - core, u], dst_ref=crecv.at[u], send_sem=c_s.at[u],
            recv_sem=c_r.at[u], device_id=var_peer(1), device_id_type=MESH,
        )

    def y_copy(u):
        return pltpu.make_async_remote_copy(
            src_ref=ysend.at[u], dst_ref=yrecv.at[u], send_sem=y_s.at[u],
            recv_sem=y_r.at[u], device_id=var_peer(2), device_id_type=MESH,
        )

    def z_copy(u):
        return pltpu.make_async_remote_copy(
            src_ref=zsend.at[u], dst_ref=zrecv.at[u], send_sem=z_s.at[u],
            recv_sem=z_r.at[u], device_id=var_peer(4 * (nz - 1 - u)), device_id_type=MESH,
        )

    def a_copy(u):
        return pltpu.make_async_remote_copy(
            src_ref=asend.at[u], dst_ref=arecv.at[u], send_sem=a_s.at[u],
            recv_sem=a_r.at[u], device_id=var_peer(4 * (nz - 1 - u)), device_id_type=MESH,
        )

    b_copy = pltpu.make_async_remote_copy(
        src_ref=bsend.at[1 - why], dst_ref=brecv, send_sem=b_s.at[0],
        recv_sem=b_r.at[0], device_id=var_peer(2), device_id_type=MESH,
    )
    first_rows = half_rows - SPLIT

    shift = jnp.sum(corr[...], axis=1, keepdims=True)
    low_lane = lax.broadcasted_iota(jnp.int32, (half_rows, LANES), 1) < LANES // 2
    tail = w[:, cut:variants]

    def step_c(u):
        cols = pl.ds(pl.multiple_of(zed_xor(nz - 1 - u) * width, width), width)
        term = acc[:, cols] + jnp.dot(tail, g[cut:variants, cols], preferred_element_type=jnp.float32)
        term = term - shift
        for t in range(2):
            top = term[0:half_rows, t * LANES : (t + 1) * LANES]
            low = term[half_rows:rows, t * LANES : (t + 1) * LANES]
            buf[0, u, t] = jnp.where(low_lane, top, pltpu.roll(low, LANES // 2, 1))
            buf[1, u, t] = jnp.where(low_lane, pltpu.roll(top, LANES // 2, 1), low)
        c_copy(u).start()

    def step_y(u):
        c_copy(u).wait()
        upper, lower = pl.ds(0, first_rows), pl.ds(first_rows, SPLIT)
        ysend[u] = buf[core, u, 1 - why, upper] + crecv[u, 1 - why, upper]
        y_copy(u).start()
        asend[u] = buf[core, u, :, lower] + crecv[u, :, lower]
        if u < nz - 1:
            a_copy(u).start()
        ykeep[u] = buf[core, u, why, upper] + crecv[u, why, upper]

    def step_z(u):
        y_copy(u).wait()
        zsend[u] = ykeep[u] + yrecv[u]
        if u < nz - 1:
            z_copy(u).start()

    for s in range(nz + 3):
        if s < nz:
            step_c(s)
        if 0 <= s - 1 < nz:
            step_y(s - 1)
        if 0 <= s - 3 < nz:
            step_z(s - 3)

    part = asend[nz - 1]
    for u in range(nz - 2, -1, -1):
        a_copy(u).wait()
        part = part + arecv[u]
    bsend[...] = part
    b_copy.start()
    res = zsend[nz - 1]
    for u in range(nz - 2, -1, -1):
        z_copy(u).wait()
        res = res + zrecv[u]
    b_copy.wait()
    res = jnp.concatenate([res, bsend[why] + brecv[...]], axis=0)
    other = pltpu.roll(res, LANES // 2, 1)
    wide = LANES // 2
    counts = other[half_rows - K : half_rows, 0:wide]
    for j in range(nv):
        src = res if j * K < half_rows else other
        at = j * K % half_rows
        out_ref[:, j, :] = src[at : at + K, 0:wide] / counts


def solution(mesh):
    nvar, nsmp = mesh.shape["var"], mesh.shape["smp"]

    def body(genotype, labels, probes, phenotype):
        variants, samples = genotype.shape
        nb = probes.shape[0]
        nv = nb + 1
        nz = nvar // 4
        chunks = variants // CHUNK
        prow = (nv + 2 + 7) // 8 * 8
        rows = (nv + 1) * K
        half = rows // 2
        f32 = jnp.float32
        dma = pltpu.SemaphoreType.DMA
        out = pl.pallas_call(
            functools.partial(kernel, nsmp, nvar),
            out_shape=jax.ShapeDtypeStruct((K, nv, LANES // 2), f32),
            in_specs=[pl.BlockSpec(memory_space=pltpu.MemorySpace.HBM)] * 4,
            out_specs=pl.BlockSpec(memory_space=pltpu.VMEM),
            scratch_shapes=[
                pltpu.VMEM((variants, samples), jnp.bfloat16),
                pltpu.VMEM((1, variants), jnp.int32),
                pltpu.VMEM((nb, samples), jnp.bfloat16),
                pltpu.VMEM((samples // LANES, LANES), jnp.bfloat16),
                pltpu.VMEM((32, samples), f32),
                pltpu.VMEM((chunks, prow, CHUNK), f32),
                pltpu.VMEM((nsmp - 1, chunks, prow, CHUNK), f32),
                pltpu.VMEM((prow, LANES), f32),
                pltpu.VMEM((nsmp - 1, prow, LANES), f32),
                pltpu.VMEM((rows, variants), jnp.bfloat16),
                pltpu.VMEM((rows, LANES), f32),
                pltpu.VMEM((rows, samples), f32),
                pltpu.VMEM((2, nz, 2, half, LANES), f32),
                pltpu.VMEM((nz, 2, half, LANES), f32),
                pltpu.VMEM((nz, half - SPLIT, LANES), f32),
                pltpu.VMEM((nz, half - SPLIT, LANES), f32),
                pltpu.VMEM((nz, half - SPLIT, LANES), f32),
                pltpu.VMEM((nz, half - SPLIT, LANES), f32),
                pltpu.VMEM((nz - 1, half - SPLIT, LANES), f32),
                pltpu.VMEM((nz, 2, SPLIT, LANES), f32),
                pltpu.VMEM((nz - 1, 2, SPLIT, LANES), f32),
                pltpu.VMEM((2, SPLIT, LANES), f32),
                pltpu.VMEM((SPLIT, LANES), f32),
                dma((chunks,)),
                dma((3,)),
                dma((nsmp - 1, chunks)),
                dma((nsmp - 1, chunks)),
                dma((nsmp - 1,)),
                dma((nsmp - 1,)),
                dma((nz,)),
                dma((nz,)),
                dma((nz,)),
                dma((nz,)),
                dma((nz - 1,)),
                dma((nz - 1,)),
                dma((nz - 1,)),
                dma((nz - 1,)),
                dma((1,)),
                dma((1,)),
                pltpu.SemaphoreType.REGULAR((max(nz - 2, 1),)),
            ],
            compiler_params=pltpu.CompilerParams(
                collective_id=0, has_side_effects=True, vmem_limit_bytes=48 << 20
            ),
        )(
            *[
                pltpu.with_memory_space_constraint(x, pltpu.HBM)
                for x in (
                    genotype,
                    labels.reshape(1, variants),
                    probes,
                    phenotype.reshape(samples // LANES, LANES),
                )
            ]
        )
        return out.reshape(K, nv, 1, LANES // 2)

    placed = (P("var", "smp"), P("var"), P(None, "smp"), P("smp"))
    return jax.shard_map(
        body, mesh=mesh, in_specs=placed, out_specs=P(None, None, "smp", "var"), check_vma=False
    )
```
